32 devices in a mesh: dp: 8 (over y, x, core), tensor: 4 (over z).
Axes of the slice: x: 2, y: 2, z: 4, core: 2. Of those that a mesh axis runs over, the one named last changes fastest.
Arguments:
- hidden_in: float32 [4096, 1024], P('dp'), may hold values from -6 to 6
- doc_ids: int32 [4096], P('dp'), may hold values from 0 to 7, never falling along the last dimension, each value on 1 to 1024 neighbouring positions
- attend_weight: bfloat16 [2, 1024, 3, 1024], P(None, 'dp', None, 'tensor'), may hold values from -0.1875 to 0.1875
- attend_bias: bfloat16 [2, 2, 1024], P(None, None, ('tensor', 'dp')), may hold values from -3 to 3
- output_weight: bfloat16 [2, 1024, 1024], P(None, ('tensor', 'dp')), may hold values from -0.75 to 0.75
- branch_bias: bfloat16 [2, 2, 1024], P(None, None, 'dp'), may hold values from -3 to 3
- expand_weight: bfloat16 [2, 1024, 4096], P(None, 'dp', 'tensor'), may hold values from -0.1875 to 0.1875
- expand_bias: bfloat16 [2, 4096], P(None, ('tensor', 'dp')), may hold values from -3 to 3
- reduce_weight: bfloat16 [2, 4096, 1024], P(None, ('tensor', 'dp')), may hold values from -0.125 to 0.125
- norm_gain: bfloat16 [2, 2, 1024], P(None, None, 'dp'), may hold values from 0.5 to 1.5
- norm_bias: bfloat16 [2, 2, 1024], P(None, None, 'dp'), may hold values from -2 to 2
- out_grad: float32 [4096, 1024], P('dp'), may hold values from -6 to 6
Outputs:
- hidden_out: float32 [4096, 1024], P('dp')
- in_grad: float32 [4096, 1024], P('dp')
- attend_wgrad: float32 [2, 1024, 3, 1024], P(None, 'dp', None, 'tensor')
- attend_bgrad: float32 [2, 2, 1024], P(None, None, ('tensor', 'dp'))
- output_wgrad: float32 [2, 1024, 1024], P(None, ('tensor', 'dp'))
- branch_bgrad: float32 [2, 2, 1024], P(None, None, 'dp')
- expand_wgrad: float32 [2, 1024, 4096], P(None, 'dp', 'tensor')
- expand_bgrad: float32 [2, 4096], P(None, ('tensor', 'dp'))
- reduce_wgrad: float32 [2, 4096, 1024], P(None, ('tensor', 'dp'))
- gain_grad: float32 [2, 2, 1024], P(None, None, 'dp')
- offset_grad: float32 [2, 2, 1024], P(None, None, 'dp')
The draws below stay inside these ranges and needn't reach their ends.
Inputs may be any that keep to these rules, and one draw needn't show every extreme that they name: doc_ids never falls from one token to the next; each of the 8 documents holds 1 to 1024 consecutive tokens, and some document exactly 1024.
All inputs are finite; a program needn't handle non-finite values.
Results may differ from the reference program's by a relative error of at most 0.025.
Values may be sent and summed in bfloat16 or wider, within the bound.
A program may use at most 192 MiB of HBM per device.

```python
import math
import jax
import jax.numpy as jnp
import numpy as np
from jax import lax

D = 1024
HEADS = 16
HEAD_DIM = 64
FF = 4096
CTX = 1024
LAYERS = 2
TOK_DEV = 512
TOKENS = 4096
BACK = 2
DOCS = 8
N_TENSOR = 4


def steps_of(own_key, dims, split, smallest, top_value):
    factor_of, own = 1.0, jax.random.fold_in(own_key, 6)
    for dim, blocks in split:
        heights = jnp.exp(jax.random.uniform(jax.random.fold_in(own, dim), (blocks,), jnp.float32, smallest / len(split), top_value / len(split)))
        factor_of = factor_of * jnp.repeat(heights, dims[dim] // blocks).reshape([-1 if axis == dim else 1 for axis in range(len(dims))])
    return factor_of


def split_up(number_of, total, most, slope):
    weights = [(1 << 20) // math.isqrt(standing ** slope) + 1 for standing in range(2, number_of + 1)]
    surplus, counts = total - most - (number_of - 1), [1] * (number_of - 1)
    while surplus > 0:
        candidates = [i for i in range(number_of - 1) if counts[i] < most]
        pool, left = sum([weights[i] for i in candidates]), surplus
        for i in candidates:
            extra = min(most - counts[i], max(1, left * weights[i] // pool), surplus)
            counts[i] = counts[i] + extra
            surplus = surplus - extra
    return np.array([most] + counts)


def uneven_parts(rng, number_of, total, bound, slope):
    if number_of == 2:
        one = jax.random.randint(rng, (), max(1, total - bound), min(bound, total - 1) + 1)
        return jnp.stack([one, total - one])
    lengths = jnp.asarray(split_up(number_of, total, bound, slope), jnp.int32)
    twos = (number_of - 1) // 2
    giver, sink = lengths[1:1 + 2 * twos:2], lengths[2:2 + 2 * twos:2]
    room = jnp.minimum(giver - 1, bound - sink)
    moved = jax.random.randint(jax.random.fold_in(rng, 1), (twos,), 0, 1 << 20) % (room + 1)
    lengths = lengths.at[1:1 + 2 * twos:2].set(giver - moved).at[2:2 + 2 * twos:2].set(sink + moved)
    return lengths[jax.random.permutation(jax.random.fold_in(rng, 2), number_of)]


def gaussian(own_key, dims, deviation, limit, cuts=(), kind=jnp.bfloat16):
    entries = deviation * jax.random.normal(own_key, dims, jnp.float32)
    if cuts:
        entries = entries * steps_of(own_key, dims, cuts, -0.22, 0.18)
    return jnp.clip(entries, -limit, limit).astype(kind)


def setup_inputs(seed: int = 0) -> dict:
    seeds = jax.random.split(jax.random.key(seed), 13)
    hidden_in = gaussian(seeds[0], (TOKENS, D), 1.0, 6.0, ((0, 8),), jnp.float32)
    doc_ids = jnp.searchsorted(jnp.cumsum(uneven_parts(seeds[1], DOCS, TOKENS, CTX, 1)), jnp.arange(TOKENS), side="right").astype(jnp.int32)
    attend_weight = gaussian(seeds[2], (LAYERS, D, 3, D), D ** -0.5, 0.1875, ((1, 8), (3, 4)))
    attend_bias = gaussian(seeds[3], (LAYERS, 2, D), 0.5, 3.0, ((2, 32),))
    output_weight = gaussian(seeds[4], (LAYERS, D, D), (D // 16) ** -0.5, 0.75, ((1, 32),))
    branch_bias = gaussian(seeds[5], (LAYERS, 2, D), 0.5, 3.0, ((2, 8),))
    expand_weight = gaussian(seeds[6], (LAYERS, D, FF), D ** -0.5, 0.1875, ((1, 8), (2, 4)))
    expand_bias = gaussian(seeds[7], (LAYERS, FF), 0.5, 3.0, ((1, 32),))
    reduce_weight = gaussian(seeds[8], (LAYERS, FF, D), (FF // 2) ** -0.5, 0.125, ((1, 32),))
    norm_gain = jnp.clip(1.0 + 0.1 * jax.random.normal(seeds[9], (LAYERS, 2, D), jnp.float32), 0.5, 1.5).astype(jnp.bfloat16)
    norm_bias = gaussian(seeds[10], (LAYERS, 2, D), 0.3, 2.0, ((2, 8),))
    out_grad = gaussian(seeds[11], (TOKENS, D), 1.0, 6.0, ((0, 8),), jnp.float32)
    return dict(hidden_in=hidden_in, doc_ids=doc_ids, attend_weight=attend_weight, attend_bias=attend_bias, output_weight=output_weight, branch_bias=branch_bias, expand_weight=expand_weight, expand_bias=expand_bias, reduce_weight=reduce_weight, norm_gain=norm_gain, norm_bias=norm_bias, out_grad=out_grad)


def contract(pattern, left_side, right_side):
    return jnp.einsum(pattern, left_side.astype(jnp.float32), right_side.astype(jnp.float32), precision=lax.Precision.HIGHEST)

def layer_norm(values, gain_row, offset_row):
    center = values - lax.optimization_barrier(jnp.mean(values, axis=-1, keepdims=True))
    spread = lax.optimization_barrier(jnp.mean(center * center, axis=-1, keepdims=True))
    return center * lax.rsqrt(spread + 1e-05) * gain_row + offset_row

def gelu_tanh(values):
    return 0.5 * values * (1.0 + jnp.tanh(0.7978845608028654 * (values + 0.044715 * values * values * values)))

def attend_forward(queries, key_block, value_block, allowed):
    factor = 1.0 / math.sqrt(queries.shape[-1])
    scores = contract('qhe,khe->hqk', queries, key_block) * factor
    unnormed = jnp.where(allowed[None], jnp.exp(scores), 0.0)
    totals = lax.optimization_barrier(jnp.sum(unnormed, axis=-1))
    probabilities = (unnormed / totals[..., None]).astype(jnp.bfloat16)
    context = contract('hqk,khe->qhe', probabilities, value_block)
    return (context.astype(jnp.bfloat16), jnp.log(totals))

def attend_backward(queries, key_block, value_block, log_totals, out_cot, allowed):
    factor = 1.0 / math.sqrt(queries.shape[-1])
    scores = contract('qhe,khe->hqk', queries, key_block) * factor
    probabilities = jnp.where(allowed[None], jnp.exp(scores - log_totals[..., None]), 0.0)
    rounded = probabilities.astype(jnp.bfloat16)
    value_cot = contract('hqk,qhe->khe', rounded, out_cot)
    prob_cot = contract('qhe,khe->hqk', out_cot, value_block)
    row_inner = lax.optimization_barrier(jnp.sum(probabilities * prob_cot, axis=-1, keepdims=True))
    score_cot = (probabilities * (prob_cot - row_inner) * factor).astype(jnp.bfloat16)
    query_cot = contract('hqk,khe->qhe', score_cot, key_block)
    key_cot = contract('hqk,qhe->khe', score_cot, queries)
    return (query_cot, key_cot, value_cot)

def group_total(partials):
    rounded = lax.optimization_barrier(partials.astype(jnp.bfloat16))
    return lax.optimization_barrier(jnp.sum(rounded.astype(jnp.float32), axis=0))

def reference(hidden_in, doc_ids, attend_weight, attend_bias, output_weight, branch_bias, expand_weight, expand_bias, reduce_weight, norm_gain, norm_bias, out_grad):
    groups = N_TENSOR
    reach_back = BACK
    block_rows = TOK_DEV
    count_blocks = TOKENS // TOK_DEV
    window_rows = (reach_back + 1) * block_rows
    head_count = HEADS
    doc_marks = doc_ids.astype(jnp.int32) + 1
    padded_marks = jnp.concatenate([jnp.zeros((reach_back * block_rows,), jnp.int32), doc_marks])
    row_ids = jnp.arange(block_rows, dtype=jnp.int32)[:, None]
    col_ids = jnp.arange(window_rows, dtype=jnp.int32)[None, :]
    causal = col_ids - reach_back * block_rows <= row_ids
    block_ids = jnp.arange(count_blocks, dtype=jnp.int32)

    def mask_of(block_index):
        own_marks = lax.dynamic_slice_in_dim(doc_marks, (block_index * block_rows).astype(jnp.int32), block_rows)
        window_marks = lax.dynamic_slice_in_dim(padded_marks, (block_index * block_rows).astype(jnp.int32), window_rows)
        return (window_marks[None, :] == own_marks[:, None]) & causal

    def pad_rows(values):
        return jnp.concatenate([jnp.zeros((reach_back * block_rows,) + values.shape[1:], values.dtype), values])

    def slice_rows(values, block_index, length):
        return lax.dynamic_slice_in_dim(values, (block_index * block_rows).astype(jnp.int32), length)
    kept_states = []
    current = hidden_in
    for layer_index in range(LAYERS):
        gain_pair = norm_gain[layer_index].astype(jnp.float32)
        offset_pair = norm_bias[layer_index].astype(jnp.float32)
        normed_one = layer_norm(current, gain_pair[0], offset_pair[0]).astype(jnp.bfloat16)
        projected = jnp.dot(normed_one, attend_weight[layer_index].reshape(D, 3 * D), preferred_element_type=jnp.float32).reshape(TOKENS, 3, D)
        bias_pair = attend_bias[layer_index].astype(jnp.float32)
        queries = (projected[:, 0] + bias_pair[0]).astype(jnp.bfloat16).reshape(TOKENS, head_count, HEAD_DIM)
        key_all = projected[:, 1].astype(jnp.bfloat16).reshape(TOKENS, head_count, HEAD_DIM)
        value_all = (projected[:, 2] + bias_pair[1]).astype(jnp.bfloat16).reshape(TOKENS, head_count, HEAD_DIM)
        key_pad = pad_rows(key_all)
        value_pad = pad_rows(value_all)

        def one_block(block_index):
            return attend_forward(slice_rows(queries, block_index, block_rows), slice_rows(key_pad, block_index, window_rows), slice_rows(value_pad, block_index, window_rows), mask_of(block_index))
        context, log_totals = lax.map(one_block, block_ids)
        flat_context = context.reshape(TOKENS, D)
        attended = group_total(contract('tgk,gkn->gtn', flat_context.reshape(TOKENS, groups, D // groups), output_weight[layer_index].reshape(groups, D // groups, D)))
        branch_pair = branch_bias[layer_index].astype(jnp.float32)
        middle = current + (attended + branch_pair[0])
        normed_two = layer_norm(middle, gain_pair[1], offset_pair[1]).astype(jnp.bfloat16)
        pre_act = jnp.dot(normed_two, expand_weight[layer_index], preferred_element_type=jnp.float32) + expand_bias[layer_index].astype(jnp.float32)
        activated = gelu_tanh(pre_act).astype(jnp.bfloat16)
        reduced = group_total(contract('tgk,gkn->gtn', activated.reshape(TOKENS, groups, FF // groups), reduce_weight[layer_index].reshape(groups, FF // groups, D)))
        output = middle + (reduced + branch_pair[1])
        kept_states.append((current, normed_one, queries, key_pad, value_pad, flat_context, log_totals, middle, normed_two, pre_act, activated))
        current = output
    hidden_out = current
    grad_now = out_grad
    layer_grads = [None] * LAYERS
    for layer_index in reversed(range(LAYERS)):
        hidden, normed_one, queries, key_pad, value_pad, flat_context, log_totals, middle, normed_two, pre_act, activated = kept_states[layer_index]
        gain_pair = norm_gain[layer_index].astype(jnp.float32)
        offset_pair = norm_bias[layer_index].astype(jnp.float32)
        bias_two = lax.optimization_barrier(jnp.sum(grad_now, axis=0))
        grad_rounded = grad_now.astype(jnp.bfloat16)
        reduce_grad = jnp.dot(activated.T, grad_rounded, preferred_element_type=jnp.float32)
        act_cot = jnp.dot(grad_rounded, reduce_weight[layer_index].T, preferred_element_type=jnp.float32)
        unused, gelu_pull = jax.vjp(gelu_tanh, pre_act)
        pre_cot = gelu_pull(act_cot)[0]
        expand_bias_grad = lax.optimization_barrier(jnp.sum(pre_cot, axis=0))
        pre_rounded = pre_cot.astype(jnp.bfloat16)
        expand_grad = jnp.dot(normed_two.T, pre_rounded, preferred_element_type=jnp.float32)
        normed_cot = group_total(contract('tgk,dgk->gtd', pre_rounded.reshape(TOKENS, groups, FF // groups), expand_weight[layer_index].reshape(D, groups, FF // groups)))
        unused, norm_pull = jax.vjp(layer_norm, middle, gain_pair[1], offset_pair[1])
        mid_part, gain_two, offset_two = norm_pull(normed_cot)
        mid_cot = grad_now + mid_part
        bias_one = lax.optimization_barrier(jnp.sum(mid_cot, axis=0))
        mid_rounded = mid_cot.astype(jnp.bfloat16)
        output_grad = jnp.dot(flat_context.T, mid_rounded, preferred_element_type=jnp.float32)
        context_cot = jnp.dot(mid_rounded, output_weight[layer_index].T, preferred_element_type=jnp.float32).astype(jnp.bfloat16).reshape(TOKENS, head_count, HEAD_DIM)

        def one_back(block_index):
            return attend_backward(slice_rows(queries, block_index, block_rows), slice_rows(key_pad, block_index, window_rows), slice_rows(value_pad, block_index, window_rows), lax.dynamic_index_in_dim(log_totals, block_index, 0, keepdims=False), slice_rows(context_cot, block_index, block_rows), mask_of(block_index))
        query_cot, key_cot, value_cot = lax.map(one_back, block_ids)
        query_cot = query_cot.reshape(TOKENS, head_count, HEAD_DIM)
        key_cot = key_cot.reshape(count_blocks, reach_back + 1, block_rows, head_count, HEAD_DIM)
        value_cot = value_cot.reshape(count_blocks, reach_back + 1, block_rows, head_count, HEAD_DIM)
        key_acc = jnp.zeros((count_blocks + reach_back, block_rows, head_count, HEAD_DIM), jnp.float32)
        value_acc = jnp.zeros((count_blocks + reach_back, block_rows, head_count, HEAD_DIM), jnp.float32)
        for hop_index in range(reach_back + 1):
            key_acc = key_acc.at[hop_index:hop_index + count_blocks].add(key_cot[:, hop_index])
            value_acc = value_acc.at[hop_index:hop_index + count_blocks].add(value_cot[:, hop_index])
        key_total = key_acc[reach_back:].reshape(TOKENS, D)
        value_total = value_acc[reach_back:].reshape(TOKENS, D)
        proj_cot = jnp.stack([query_cot.reshape(TOKENS, D), key_total, value_total], axis=1)
        attend_bias_grad = jnp.stack([lax.optimization_barrier(jnp.sum(proj_cot[:, 0], axis=0)), lax.optimization_barrier(jnp.sum(proj_cot[:, 2], axis=0))])
        proj_rounded = proj_cot.astype(jnp.bfloat16)
        attend_grad = jnp.dot(normed_one.T, proj_rounded.reshape(TOKENS, 3 * D), preferred_element_type=jnp.float32).reshape(D, 3, D)
        normed_cot_one = group_total(contract('tcgk,dcgk->gtd', proj_rounded.reshape(TOKENS, 3, groups, D // groups), attend_weight[layer_index].reshape(D, 3, groups, D // groups)))
        unused, first_pull = jax.vjp(layer_norm, hidden, gain_pair[0], offset_pair[0])
        hid_part, gain_one, offset_one = first_pull(normed_cot_one)
        grad_now = mid_cot + hid_part
        layer_grads[layer_index] = (attend_grad, attend_bias_grad, output_grad, jnp.stack([bias_one, bias_two]), expand_grad, expand_bias_grad, reduce_grad, jnp.stack([gain_one, gain_two]), jnp.stack([offset_one, offset_two]))
    stacked = [jnp.stack([entry[member] for entry in layer_grads]) for member in range(9)]
    return (hidden_out, grad_now, stacked[0], stacked[1], stacked[2], stacked[3], stacked[4], stacked[5], stacked[6], stacked[7], stacked[8])
```

```python
import functools
import math

import jax
import jax.numpy as jnp
from jax import lax
from jax.experimental import pallas as pl
from jax.experimental.pallas import tpu as pltpu
from jax.sharding import PartitionSpec as P

HEAD_DIM = 64
CTX = 1024
LANES = 128
ROW_TILE = 256


def passed_along(block, axis, distance):
    devices = range(lax.axis_size(axis))
    route = [(i - distance, i) for i in devices if i - distance in devices]
    return lax.ppermute(block, axis, route)


def contract(pattern, left_side, right_side):
    return jnp.einsum(pattern, left_side, right_side, preferred_element_type=jnp.float32)


def layer_norm(values, gain_row, offset_row):
    center = values - jnp.mean(values, axis=-1, keepdims=True)
    spread = jnp.mean(center * center, axis=-1, keepdims=True)
    return center * lax.rsqrt(spread + 1e-05) * gain_row + offset_row


def gelu_tanh(values):
    return (
        0.5
        * values
        * (1.0 + jnp.tanh(0.7978845608028654 * (values + 0.044715 * values * values * values)))
    )


def dot_rows(left_side, right_side):
    return lax.dot_general(
        left_side, right_side, (((1,), (1,)), ((), ())), preferred_element_type=jnp.float32
    )


def dot_tokens(left_side, right_side):
    return lax.dot_general(
        left_side, right_side, (((0,), (0,)), ((), ())), preferred_element_type=jnp.float32
    )


def row_tiles(rows, window_rows):
    tile = min(ROW_TILE, rows)
    back = window_rows - rows
    for start in range(0, rows, tile):
        low = max(0, (back + start - CTX + 1) // LANES * LANES)
        yield start, tile, low, back + start + tile


def tile_mask(own_ref, window_ref, start, tile, low, high, back):
    own = own_ref[start : start + tile, :]
    window = window_ref[:, low:high]
    row = lax.broadcasted_iota(jnp.int32, (tile, high - low), 0) + (start + back)
    col = lax.broadcasted_iota(jnp.int32, (tile, high - low), 1) + low
    return (window == own) & (col <= row)


def head_parts(width):
    group = min(LANES, width)
    for base in range(0, width, group):
        for inner in range(0, group, HEAD_DIM):
            yield base, group, inner


def pick(block, inner):
    lane = lax.broadcasted_iota(jnp.int32, block.shape, 1)
    return jnp.where((lane >= inner) & (lane < inner + HEAD_DIM), block, jnp.zeros_like(block))


def forward_kernel(q_ref, kv_ref, own_ref, window_ref, o_ref, lse_ref):
    rows, width = q_ref.shape
    window_rows = kv_ref.shape[0]
    back = window_rows - rows
    factor = 1.0 / math.sqrt(HEAD_DIM)
    for start, tile, low, high in row_tiles(rows, window_rows):
        allowed = tile_mask(own_ref, window_ref, start, tile, low, high, back)
        held = None
        logs = []
        for base, group, inner in head_parts(width):
            queries = pick(q_ref[start : start + tile, base : base + group], inner)
            keys = kv_ref[low:high, base : base + group]
            values = kv_ref[low:high, width + base : width + base + group]
            unnormed = jnp.where(allowed, jnp.exp(dot_rows(queries, keys) * factor), 0.0)
            totals = jnp.sum(unnormed, axis=-1, keepdims=True)
            probabilities = (unnormed * (1.0 / totals)).astype(jnp.bfloat16)
            context = pick(
                jnp.dot(probabilities, values, preferred_element_type=jnp.float32), inner
            )
            held = context if inner == 0 else held + context
            logs.append(jnp.log(totals))
            if inner + HEAD_DIM == group:
                o_ref[start : start + tile, base : base + group] = held.astype(jnp.bfloat16)
        for index, entry in enumerate(logs):
            lse_ref[start : start + tile, index : index + 1] = entry


def backward_kernel(
    q_ref, kv_ref, lse_ref, cot_ref, own_ref, window_ref, dq_ref, own_out, back_out, acc
):
    rows, width = q_ref.shape
    window_rows = kv_ref.shape[0]
    back = window_rows - rows
    factor = 1.0 / math.sqrt(HEAD_DIM)
    acc[...] = jnp.zeros_like(acc)
    for start, tile, low, high in row_tiles(rows, window_rows):
        allowed = tile_mask(own_ref, window_ref, start, tile, low, high, back)
        held = None
        for index, (base, group, inner) in enumerate(head_parts(width)):
            queries = pick(q_ref[start : start + tile, base : base + group], inner)
            cots = pick(cot_ref[start : start + tile, base : base + group], inner)
            keys = kv_ref[low:high, base : base + group]
            values = kv_ref[low:high, width + base : width + base + group]
            logs = lse_ref[start : start + tile, index : index + 1]
            scores = dot_rows(queries, keys) * factor
            probabilities = jnp.where(allowed, jnp.exp(scores - logs), 0.0)
            rounded = probabilities.astype(jnp.bfloat16)
            acc[low:high, width + base : width + base + group] += dot_tokens(rounded, cots)
            prob_cot = dot_rows(cots, values)
            inner_sum = jnp.sum(probabilities * prob_cot, axis=-1, keepdims=True)
            score_cot = (probabilities * (prob_cot - inner_sum) * factor).astype(jnp.bfloat16)
            acc[low:high, base : base + group] += dot_tokens(score_cot, queries)
            part = pick(jnp.dot(score_cot, keys, preferred_element_type=jnp.float32), inner)
            held = part if inner == 0 else held + part
            if inner + HEAD_DIM == group:
                dq_ref[start : start + tile, base : base + group] = held
    own_out[...] = acc[back:, :]
    back_out[...] = acc[:back, :].astype(jnp.bfloat16)


def in_vmem(count):
    return [pl.BlockSpec(memory_space=pltpu.VMEM)] * count


def attend_forward(queries, window_kv, own_marks, window_marks):
    rows, width = queries.shape
    return pl.pallas_call(
        forward_kernel,
        out_shape=(
            jax.ShapeDtypeStruct((rows, width), jnp.bfloat16),
            jax.ShapeDtypeStruct((rows, width // HEAD_DIM), jnp.float32),
        ),
        in_specs=in_vmem(4),
        out_specs=tuple(in_vmem(2)),
        compiler_params=pltpu.CompilerParams(vmem_limit_bytes=40 * 1024 * 1024),
        name="attend_forward",
    )(queries, window_kv, own_marks, window_marks)


def attend_backward(queries, window_kv, log_totals, out_cot, own_marks, window_marks):
    rows, width = queries.shape
    window_rows = window_kv.shape[0]
    return pl.pallas_call(
        backward_kernel,
        out_shape=(
            jax.ShapeDtypeStruct((rows, width), jnp.float32),
            jax.ShapeDtypeStruct((rows, 2 * width), jnp.float32),
            jax.ShapeDtypeStruct((window_rows - rows, 2 * width), jnp.bfloat16),
        ),
        in_specs=in_vmem(6),
        out_specs=tuple(in_vmem(3)),
        scratch_shapes=[pltpu.VMEM((window_rows, 2 * width), jnp.float32)],
        compiler_params=pltpu.CompilerParams(vmem_limit_bytes=48 * 1024 * 1024),
        name="attend_backward",
    )(queries, window_kv, log_totals, out_cot, own_marks, window_marks)


def tensor_total(partial_value):
    return lax.psum(partial_value.astype(jnp.bfloat16), "tensor").astype(jnp.float32)


def forward_layer(hidden, params, marks, reach_back):
    attend_w, attend_b, output_w, branches, expand_w, expand_b, reduce_w, gains, offsets = params
    width = output_w.shape[0]
    own_marks, window_marks = marks
    normed_one = layer_norm(hidden, gains[0], offsets[0]).astype(jnp.bfloat16)
    projected = jnp.dot(normed_one, attend_w, preferred_element_type=jnp.float32)
    queries = (projected[:, :width] + attend_b[0]).astype(jnp.bfloat16)
    kv_bias = jnp.concatenate([jnp.zeros_like(attend_b[1]), attend_b[1]])
    kv_now = (projected[:, width:] + kv_bias).astype(jnp.bfloat16)
    kv_list = [passed_along(kv_now, "dp", hop) for hop in range(reach_back, 0, -1)]
    window_kv = jnp.concatenate(kv_list + [kv_now], axis=0)
    context, log_totals = attend_forward(queries, window_kv, own_marks, window_marks)
    attended = tensor_total(jnp.dot(context, output_w, preferred_element_type=jnp.float32))
    middle = hidden + (attended + branches[0])
    normed_two = layer_norm(middle, gains[1], offsets[1]).astype(jnp.bfloat16)
    pre_act = jnp.dot(normed_two, expand_w, preferred_element_type=jnp.float32) + expand_b
    activated = gelu_tanh(pre_act).astype(jnp.bfloat16)
    reduced = tensor_total(jnp.dot(activated, reduce_w, preferred_element_type=jnp.float32))
    output = middle + (reduced + branches[1])
    kept_state = (
        hidden,
        normed_one,
        queries,
        window_kv,
        context,
        log_totals,
        middle,
        normed_two,
        pre_act,
        activated,
    )
    return (output, kept_state)


def backward_layer(grad_out, params, kept_state, marks, reach_back):
    attend_w, attend_b, output_w, branches, expand_w, expand_b, reduce_w, gains, offsets = params
    (
        hidden,
        normed_one,
        queries,
        window_kv,
        context,
        log_totals,
        middle,
        normed_two,
        pre_act,
        activated,
    ) = kept_state
    own_marks, window_marks = marks
    rows = hidden.shape[0]
    width = output_w.shape[0]
    bias_two = jnp.sum(grad_out, axis=0)
    grad_rounded = grad_out.astype(jnp.bfloat16)
    act_cot = contract("td,fd->tf", grad_rounded, reduce_w)
    unused, gelu_pull = jax.vjp(gelu_tanh, pre_act)
    pre_cot = gelu_pull(act_cot)[0]
    expand_bias_grad = jnp.sum(pre_cot, axis=0)
    pre_rounded = pre_cot.astype(jnp.bfloat16)
    normed_cot = tensor_total(contract("tf,df->td", pre_rounded, expand_w))
    reduce_grad = contract("tf,td->fd", activated, grad_rounded).astype(jnp.bfloat16)
    expand_grad = contract("td,tf->df", normed_two, pre_rounded).astype(jnp.bfloat16)
    unused, norm_pull = jax.vjp(layer_norm, middle, gains[1], offsets[1])
    mid_part, gain_two, offset_two = norm_pull(normed_cot)
    mid_cot = grad_out + mid_part
    bias_one = jnp.sum(mid_cot, axis=0)
    mid_rounded = mid_cot.astype(jnp.bfloat16)
    output_grad = contract("tk,td->kd", context, mid_rounded).astype(jnp.bfloat16)
    context_cot = contract("td,kd->tk", mid_rounded, output_w).astype(jnp.bfloat16)
    query_cot, kv_own, kv_back = attend_backward(
        queries, window_kv, log_totals, context_cot, own_marks, window_marks
    )
    for hop in range(1, reach_back + 1):
        begin = (reach_back - hop) * rows
        kv_own = kv_own + passed_along(kv_back[begin : begin + rows], "dp", -hop).astype(
            jnp.float32
        )
    attend_bias_grad = jnp.stack([jnp.sum(query_cot, axis=0), jnp.sum(kv_own[:, width:], axis=0)])
    proj_rounded = jnp.concatenate(
        [query_cot.astype(jnp.bfloat16), kv_own.astype(jnp.bfloat16)], axis=1
    )
    normed_cot_one = tensor_total(contract("tc,dc->td", proj_rounded, attend_w))
    attend_grad = contract("td,tc->dc", normed_one, proj_rounded).astype(jnp.bfloat16)
    unused, first_pull = jax.vjp(layer_norm, hidden, gains[0], offsets[0])
    hid_part, gain_one, offset_one = first_pull(normed_cot_one)
    in_cot = mid_cot + hid_part
    small = (
        attend_bias_grad,
        jnp.stack([bias_one, bias_two]),
        expand_bias_grad,
        jnp.stack([gain_one, gain_two]),
        jnp.stack([offset_one, offset_two]),
    )
    return (in_cot, expand_grad, reduce_grad, attend_grad, output_grad, small)


def scattered(block):
    return lax.psum_scatter(block, "dp", scatter_dimension=0, tiled=True)


def pack_output(block, model, share):
    part = model // lax.axis_size("dp")
    slabs = part // share
    owners = block.shape[0] // share
    return (
        block.reshape(owners, share, slabs, model // slabs)
        .transpose(0, 2, 1, 3)
        .reshape(owners * part, model // slabs)
    )


def unpack_output(block, model, share):
    part = model // lax.axis_size("dp")
    slabs = part // share
    owners = block.shape[0] // part
    return (
        block.reshape(owners, slabs, share, model // slabs)
        .transpose(0, 2, 1, 3)
        .reshape(owners * share, model)
    )


def split_owned(pieces, sizes, size):
    rows = [
        jnp.moveaxis(p.reshape(p.shape[:-1] + (size, p.shape[-1] // size)), -2, 0).reshape(size, -1)
        for p in pieces
    ]
    return jnp.concatenate(rows, axis=1)


def local(
    hidden_in,
    doc_ids,
    attend_weight,
    attend_bias,
    output_weight,
    branch_bias,
    expand_weight,
    expand_bias,
    reduce_weight,
    norm_gain,
    norm_bias,
    out_grad,
):
    size = lax.axis_size("dp")
    layer_count, part, three, width = attend_weight.shape
    tok_rows, model = hidden_in.shape
    share = output_weight.shape[1]
    unit_share = reduce_weight.shape[1]
    hidden_units = expand_weight.shape[2]
    reach_back = (CTX + tok_rows - 2) // tok_rows
    own_row = doc_ids + 1
    mark_list = [passed_along(own_row, "dp", hop) for hop in range(reach_back, 0, -1)]
    marks = (own_row[:, None], jnp.concatenate(mark_list + [own_row])[None, :])

    small_in = (attend_bias, branch_bias, expand_bias, norm_gain, norm_bias)
    flat = jnp.concatenate([entry.reshape(-1) for entry in small_in])
    flat_all = lax.all_gather(flat[None], "dp", axis=0, tiled=True)
    small_full = []
    at = 0
    for entry in small_in:
        piece = flat_all[:, at : at + entry.size].reshape((size,) + entry.shape)
        at += entry.size
        piece = jnp.moveaxis(piece, 0, -2)
        small_full.append(
            piece.reshape(entry.shape[:-1] + (size * entry.shape[-1],)).astype(jnp.float32)
        )
    attend_b, branches, expand_b, gains, offsets = small_full

    params = []
    for layer in range(layer_count):
        first = lax.all_gather(
            jnp.concatenate(
                [
                    attend_weight[layer].reshape(part, three * width),
                    pack_output(output_weight[layer], model, share),
                ],
                axis=1,
            ),
            "dp",
            axis=0,
            tiled=True,
        )
        second = lax.all_gather(
            jnp.concatenate(
                [expand_weight[layer], pack_output(reduce_weight[layer], model, unit_share)],
                axis=1,
            ),
            "dp",
            axis=0,
            tiled=True,
        )
        params.append(
            (
                first[:, : three * width],
                attend_b[layer],
                unpack_output(first[:, three * width :], model, share),
                branches[layer],
                second[:, :hidden_units],
                expand_b[layer],
                unpack_output(second[:, hidden_units:], model, unit_share),
                gains[layer],
                offsets[layer],
            )
        )
    saved = []
    current = hidden_in
    for layer in range(layer_count):
        current, kept_state = forward_layer(current, params[layer], marks, reach_back)
        saved.append(kept_state)
    grad_now = out_grad
    hidden_list = [None] * layer_count
    attend_list = [None] * layer_count
    small_list = [None] * layer_count
    for layer in reversed(range(layer_count)):
        grad_now, expand_grad, reduce_grad, attend_grad, output_grad, small = backward_layer(
            grad_now, params[layer], saved[layer], marks, reach_back
        )
        hidden_list[layer] = scattered(
            jnp.concatenate([expand_grad, pack_output(reduce_grad, model, unit_share)], axis=1)
        )
        small_list[layer] = small
        blocks = [attend_grad, pack_output(output_grad, model, share)]
        if layer == 0:
            stacked = [jnp.stack([entry[i] for entry in small_list]) for i in range(len(small))]
            flat_rows = split_owned(stacked, None, size).astype(jnp.bfloat16)
            count = flat_rows.shape[1]
            room = part * LANES * (-(-count // (part * LANES)))
            padded = jnp.pad(flat_rows, ((0, 0), (0, room - count)))
            blocks.append(padded.reshape(size * part, room // part))
        attend_list[layer] = scattered(jnp.concatenate(blocks, axis=1))
    hidden_out = [entry.astype(jnp.float32) for entry in hidden_list]
    attend_out = [entry.astype(jnp.float32) for entry in attend_list]
    fold = three * width
    slab = model * share // part
    tail = attend_out[0][:, fold + slab :].reshape(-1)
    small_out = []
    at = 0
    for entry in small_in:
        small_out.append(tail[at : at + entry.size].reshape(entry.shape))
        at += entry.size
    attend_bgrad, branch_bgrad, expand_bgrad, gain_grad, offset_grad = small_out
    return (
        current,
        grad_now,
        jnp.stack([entry[:, :fold].reshape(part, three, width) for entry in attend_out]),
        attend_bgrad,
        jnp.stack([unpack_output(entry[:, fold : fold + slab], model, share) for entry in attend_out]),
        branch_bgrad,
        jnp.stack([entry[:, :hidden_units] for entry in hidden_out]),
        expand_bgrad,
        jnp.stack(
            [unpack_output(entry[:, hidden_units:], model, unit_share) for entry in hidden_out]
        ),
        gain_grad,
        offset_grad,
    )


def solution(mesh):
    return jax.shard_map(
        local,
        mesh=mesh,
        in_specs=(
            P("dp", None),
            P("dp"),
            P(None, "dp", None, "tensor"),
            P(None, None, ("tensor", "dp")),
            P(None, ("tensor", "dp"), None),
            P(None, None, "dp"),
            P(None, "dp", "tensor"),
            P(None, ("tensor", "dp")),
            P(None, ("tensor", "dp"), None),
            P(None, None, "dp"),
            P(None, None, "dp"),
            P("dp", None),
        ),
        out_specs=(
            P("dp", None),
            P("dp", None),
            P(None, "dp", None, "tensor"),
            P(None, None, ("tensor", "dp")),
            P(None, ("tensor", "dp"), None),
            P(None, None, "dp"),
            P(None, "dp", "tensor"),
            P(None, ("tensor", "dp")),
            P(None, ("tensor", "dp"), None),
            P(None, None, "dp"),
            P(None, None, "dp"),
        ),
        check_vma=False,
    )
```

```python
import functools
import math

import jax
import jax.numpy as jnp
from jax import lax
from jax.experimental import pallas as pl
from jax.experimental.pallas import tpu as pltpu
from jax.sharding import PartitionSpec as P

HEAD_DIM = 64
CTX = 1024
LANES = 128
ROW_TILE = 256


def passed_along(block, axis, distance):
    devices = range(lax.axis_size(axis))
    route = [(i - distance, i) for i in devices if i - distance in devices]
    return lax.ppermute(block, axis, route)


def contract(pattern, left_side, right_side):
    return jnp.einsum(pattern, left_side, right_side, preferred_element_type=jnp.float32)


def layer_norm(values, gain_row, offset_row):
    center = values - jnp.mean(values, axis=-1, keepdims=True)
    spread = jnp.mean(center * center, axis=-1, keepdims=True)
    return center * lax.rsqrt(spread + 1e-05) * gain_row + offset_row


def gelu_tanh(values):
    return (
        0.5
        * values
        * (1.0 + jnp.tanh(0.7978845608028654 * (values + 0.044715 * values * values * values)))
    )


def dot_rows(left_side, right_side):
    return lax.dot_general(
        left_side, right_side, (((1,), (1,)), ((), ())), preferred_element_type=jnp.float32
    )


def dot_tokens(left_side, right_side):
    return lax.dot_general(
        left_side, right_side, (((0,), (0,)), ((), ())), preferred_element_type=jnp.float32
    )


def row_tiles(rows, window_rows):
    tile = min(ROW_TILE, rows)
    back = window_rows - rows
    for start in range(0, rows, tile):
        low = max(0, (back + start - CTX + 1) // LANES * LANES)
        yield start, tile, low, back + start + tile


def tile_mask(own_ref, window_ref, start, tile, low, high, back):
    own = own_ref[start : start + tile, :]
    window = window_ref[:, low:high]
    row = lax.broadcasted_iota(jnp.int32, (tile, high - low), 0) + (start + back)
    col = lax.broadcasted_iota(jnp.int32, (tile, high - low), 1) + low
    return (window == own) & (col <= row)


def head_parts(width):
    group = min(LANES, width)
    for base in range(0, width, group):
        for inner in range(0, group, HEAD_DIM):
            yield base, group, inner


def pick(block, inner):
    lane = lax.broadcasted_iota(jnp.int32, block.shape, 1)
    return jnp.where((lane >= inner) & (lane < inner + HEAD_DIM), block, jnp.zeros_like(block))


def forward_kernel(q_ref, kv_ref, own_ref, window_ref, o_ref, lse_ref):
    rows, width = q_ref.shape
    window_rows = kv_ref.shape[0]
    back = window_rows - rows
    factor = 1.0 / math.sqrt(HEAD_DIM)
    for start, tile, low, high in row_tiles(rows, window_rows):
        allowed = tile_mask(own_ref, window_ref, start, tile, low, high, back)
        held = None
        logs = []
        for base, group, inner in head_parts(width):
            queries = pick(q_ref[start : start + tile, base : base + group], inner)
            keys = kv_ref[low:high, base : base + group]
            values = kv_ref[low:high, width + base : width + base + group]
            unnormed = jnp.where(allowed, jnp.exp(dot_rows(queries, keys) * factor), 0.0)
            totals = jnp.sum(unnormed, axis=-1, keepdims=True)
            probabilities = (unnormed * (1.0 / totals)).astype(jnp.bfloat16)
            context = pick(
                jnp.dot(probabilities, values, preferred_element_type=jnp.float32), inner
            )
            held = context if inner == 0 else held + context
            logs.append(jnp.log(totals))
            if inner + HEAD_DIM == group:
                o_ref[start : start + tile, base : base + group] = held.astype(jnp.bfloat16)
        for index, entry in enumerate(logs):
            lse_ref[start : start + tile, index : index + 1] = entry


def backward_kernel(
    q_ref, kv_ref, lse_ref, cot_ref, own_ref, window_ref, dq_ref, own_out, back_out, acc
):
    rows, width = q_ref.shape
    window_rows = kv_ref.shape[0]
    back = window_rows - rows
    factor = 1.0 / math.sqrt(HEAD_DIM)
    acc[...] = jnp.zeros_like(acc)
    for start, tile, low, high in row_tiles(rows, window_rows):
        allowed = tile_mask(own_ref, window_ref, start, tile, low, high, back)
        held = None
        for index, (base, group, inner) in enumerate(head_parts(width)):
            queries = pick(q_ref[start : start + tile, base : base + group], inner)
            cots = pick(cot_ref[start : start + tile, base : base + group], inner)
            keys = kv_ref[low:high, base : base + group]
            values = kv_ref[low:high, width + base : width + base + group]
            logs = lse_ref[start : start + tile, index : index + 1]
            scores = dot_rows(queries, keys) * factor
            probabilities = jnp.where(allowed, jnp.exp(scores - logs), 0.0)
            rounded = probabilities.astype(jnp.bfloat16)
            acc[low:high, width + base : width + base + group] += dot_tokens(rounded, cots)
            prob_cot = dot_rows(cots, values)
            inner_sum = jnp.sum(probabilities * prob_cot, axis=-1, keepdims=True)
            score_cot = (probabilities * (prob_cot - inner_sum) * factor).astype(jnp.bfloat16)
            acc[low:high, base : base + group] += dot_tokens(score_cot, queries)
            part = pick(jnp.dot(score_cot, keys, preferred_element_type=jnp.float32), inner)
            held = part if inner == 0 else held + part
            if inner + HEAD_DIM == group:
                dq_ref[start : start + tile, base : base + group] = held
    own_out[...] = acc[back:, :]
    back_out[...] = acc[:back, :].astype(jnp.bfloat16)


def in_vmem(count):
    return [pl.BlockSpec(memory_space=pltpu.VMEM)] * count


def attend_forward(queries, window_kv, own_marks, window_marks):
    rows, width = queries.shape
    return pl.pallas_call(
        forward_kernel,
        out_shape=(
            jax.ShapeDtypeStruct((rows, width), jnp.bfloat16),
            jax.ShapeDtypeStruct((rows, width // HEAD_DIM), jnp.float32),
        ),
        in_specs=in_vmem(4),
        out_specs=tuple(in_vmem(2)),
        compiler_params=pltpu.CompilerParams(vmem_limit_bytes=40 * 1024 * 1024),
        name="attend_forward",
    )(queries, window_kv, own_marks, window_marks)


def attend_backward(queries, window_kv, log_totals, out_cot, own_marks, window_marks):
    rows, width = queries.shape
    window_rows = window_kv.shape[0]
    return pl.pallas_call(
        backward_kernel,
        out_shape=(
            jax.ShapeDtypeStruct((rows, width), jnp.float32),
            jax.ShapeDtypeStruct((rows, 2 * width), jnp.float32),
            jax.ShapeDtypeStruct((window_rows - rows, 2 * width), jnp.bfloat16),
        ),
        in_specs=in_vmem(6),
        out_specs=tuple(in_vmem(3)),
        scratch_shapes=[pltpu.VMEM((window_rows, 2 * width), jnp.float32)],
        compiler_params=pltpu.CompilerParams(vmem_limit_bytes=48 * 1024 * 1024),
        name="attend_backward",
    )(queries, window_kv, log_totals, out_cot, own_marks, window_marks)


def line_kernel(chunks, x_ref, o_ref, from_near, from_mid, pair, total, near_send, mid_send, near_recv, mid_recv):
    place = lax.axis_index("tensor")
    near = place + 1 - 2 * lax.rem(place, 2)
    across = 3 - place
    is_end = (place == 0) | (place == 3)
    is_mid = (place == 1) | (place == 2)
    step = x_ref.shape[0] // chunks
    barrier = pltpu.get_barrier_semaphore()

    def part(ref, c):
        return ref.at[pl.ds(c * step, step)]

    def to_near(src, c):
        return pltpu.make_async_remote_copy(
            src_ref=part(src, c),
            dst_ref=part(from_near, c),
            send_sem=near_send.at[c],
            recv_sem=near_recv.at[c],
            device_id={"tensor": near},
            device_id_type=pl.DeviceIdType.MESH,
        )

    def to_mid(c):
        return pltpu.make_async_remote_copy(
            src_ref=part(pair, c),
            dst_ref=part(from_mid, c),
            send_sem=mid_send.at[c],
            recv_sem=mid_recv.at[c],
            device_id={"tensor": across},
            device_id_type=pl.DeviceIdType.MESH,
        )

    def added(left, right, c):
        rows = pl.ds(c * step, step)
        both = left[rows, :].astype(jnp.float32) + right[rows, :].astype(jnp.float32)
        return both.astype(jnp.bfloat16)

    pl.semaphore_signal(
        barrier, inc=1, device_id={"tensor": near}, device_id_type=pl.DeviceIdType.MESH
    )

    @pl.when(is_end)
    def _():
        pl.semaphore_wait(barrier, 1)
        for c in range(chunks):
            to_near(x_ref, c).start()
        for c in range(chunks):
            to_near(x_ref, c).wait_recv()
            rows = pl.ds(c * step, step)
            o_ref[rows, :] = from_near[rows, :]
        for c in range(chunks):
            to_near(x_ref, c).wait_send()

    @pl.when(is_mid)
    def _():
        pl.semaphore_signal(
            barrier, inc=1, device_id={"tensor": across}, device_id_type=pl.DeviceIdType.MESH
        )
        pl.semaphore_wait(barrier, 2)
        lag = 2
        for c in range(chunks + lag):
            if c < chunks:
                to_near(total, c).wait_recv()
                pair[pl.ds(c * step, step), :] = added(x_ref, from_near, c)
                to_mid(c).start()
            done = c - lag
            if done >= 0:
                to_mid(done).wait_recv()
                result = added(pair, from_mid, done)
                total[pl.ds(done * step, step), :] = result
                to_near(total, done).start()
                o_ref[pl.ds(done * step, step), :] = result
        for c in range(chunks):
            to_mid(c).wait_send()
            to_near(total, c).wait_send()


def tensor_total(partial_value):
    rounded = partial_value.astype(jnp.bfloat16)
    rows = rounded.shape[0]
    if lax.axis_size("tensor") != 4 or rows % 128:
        return lax.psum(rounded, "tensor").astype(jnp.float32)
    chunks = 8
    block = pltpu.VMEM(rounded.shape, jnp.bfloat16)
    summed = pl.pallas_call(
        functools.partial(line_kernel, chunks),
        out_shape=jax.ShapeDtypeStruct(rounded.shape, jnp.bfloat16),
        in_specs=in_vmem(1),
        out_specs=in_vmem(1)[0],
        scratch_shapes=[block] * 4 + [pltpu.SemaphoreType.DMA((chunks,))] * 4,
        compiler_params=pltpu.CompilerParams(
            collective_id=0, has_side_effects=True, vmem_limit_bytes=24 * 1024 * 1024
        ),
        name="line_total",
    )(rounded)
    return summed.astype(jnp.float32)


def forward_layer(hidden, params, marks, reach_back):
    attend_w, attend_b, output_w, branches, expand_w, expand_b, reduce_w, gains, offsets = params
    width = output_w.shape[0]
    own_marks, window_marks = marks
    normed_one = layer_norm(hidden, gains[0], offsets[0]).astype(jnp.bfloat16)
    projected = jnp.dot(normed_one, attend_w, preferred_element_type=jnp.float32)
    queries = (projected[:, :width] + attend_b[0]).astype(jnp.bfloat16)
    kv_bias = jnp.concatenate([jnp.zeros_like(attend_b[1]), attend_b[1]])
    kv_now = (projected[:, width:] + kv_bias).astype(jnp.bfloat16)
    kv_list = [passed_along(kv_now, "dp", hop) for hop in range(reach_back, 0, -1)]
    window_kv = jnp.concatenate(kv_list + [kv_now], axis=0)
    context, log_totals = attend_forward(queries, window_kv, own_marks, window_marks)
    attended = tensor_total(jnp.dot(context, output_w, preferred_element_type=jnp.float32))
    middle = hidden + (attended + branches[0])
    normed_two = layer_norm(middle, gains[1], offsets[1]).astype(jnp.bfloat16)
    pre_act = jnp.dot(normed_two, expand_w, preferred_element_type=jnp.float32) + expand_b
    activated = gelu_tanh(pre_act).astype(jnp.bfloat16)
    reduced = tensor_total(jnp.dot(activated, reduce_w, preferred_element_type=jnp.float32))
    output = middle + (reduced + branches[1])
    kept_state = (
        hidden,
        normed_one,
        queries,
        window_kv,
        context,
        log_totals,
        middle,
        normed_two,
        pre_act,
        activated,
    )
    return (output, kept_state)


def backward_layer(grad_out, params, kept_state, marks, reach_back):
    attend_w, attend_b, output_w, branches, expand_w, expand_b, reduce_w, gains, offsets = params
    (
        hidden,
        normed_one,
        queries,
        window_kv,
        context,
        log_totals,
        middle,
        normed_two,
        pre_act,
        activated,
    ) = kept_state
    own_marks, window_marks = marks
    rows = hidden.shape[0]
    width = output_w.shape[0]
    bias_two = jnp.sum(grad_out, axis=0)
    grad_rounded = grad_out.astype(jnp.bfloat16)
    act_cot = contract("td,fd->tf", grad_rounded, reduce_w)
    unused, gelu_pull = jax.vjp(gelu_tanh, pre_act)
    pre_cot = gelu_pull(act_cot)[0]
    expand_bias_grad = jnp.sum(pre_cot, axis=0)
    pre_rounded = pre_cot.astype(jnp.bfloat16)
    normed_cot = tensor_total(contract("tf,df->td", pre_rounded, expand_w))
    reduce_grad = contract("tf,td->fd", activated, grad_rounded).astype(jnp.bfloat16)
    expand_grad = contract("td,tf->df", normed_two, pre_rounded).astype(jnp.bfloat16)
    unused, norm_pull = jax.vjp(layer_norm, middle, gains[1], offsets[1])
    mid_part, gain_two, offset_two = norm_pull(normed_cot)
    mid_cot = grad_out + mid_part
    bias_one = jnp.sum(mid_cot, axis=0)
    mid_rounded = mid_cot.astype(jnp.bfloat16)
    output_grad = contract("tk,td->kd", context, mid_rounded).astype(jnp.bfloat16)
    context_cot = contract("td,kd->tk", mid_rounded, output_w).astype(jnp.bfloat16)
    context_cot, expand_grad, reduce_grad = lax.optimization_barrier(
        (context_cot, expand_grad, reduce_grad)
    )
    query_cot, kv_own, kv_back = attend_backward(
        queries, window_kv, log_totals, context_cot, own_marks, window_marks
    )
    for hop in range(1, reach_back + 1):
        begin = (reach_back - hop) * rows
        kv_own = kv_own + passed_along(kv_back[begin : begin + rows], "dp", -hop).astype(
            jnp.float32
        )
    attend_bias_grad = jnp.stack([jnp.sum(query_cot, axis=0), jnp.sum(kv_own[:, width:], axis=0)])
    proj_rounded = jnp.concatenate(
        [query_cot.astype(jnp.bfloat16), kv_own.astype(jnp.bfloat16)], axis=1
    )
    normed_cot_one = tensor_total(contract("tc,dc->td", proj_rounded, attend_w))
    attend_grad = contract("td,tc->dc", normed_one, proj_rounded).astype(jnp.bfloat16)
    unused, first_pull = jax.vjp(layer_norm, hidden, gains[0], offsets[0])
    hid_part, gain_one, offset_one = first_pull(normed_cot_one)
    in_cot = mid_cot + hid_part
    small = (
        attend_bias_grad,
        jnp.stack([bias_one, bias_two]),
        expand_bias_grad,
        jnp.stack([gain_one, gain_two]),
        jnp.stack([offset_one, offset_two]),
    )
    return (in_cot, expand_grad, reduce_grad, attend_grad, output_grad, small)


def scattered(block):
    return lax.psum_scatter(block, "dp", scatter_dimension=0, tiled=True)


def pack_output(block, model, share):
    part = model // lax.axis_size("dp")
    slabs = part // share
    owners = block.shape[0] // share
    return (
        block.reshape(owners, share, slabs, model // slabs)
        .transpose(0, 2, 1, 3)
        .reshape(owners * part, model // slabs)
    )


def unpack_output(block, model, share):
    part = model // lax.axis_size("dp")
    slabs = part // share
    owners = block.shape[0] // part
    return (
        block.reshape(owners, slabs, share, model // slabs)
        .transpose(0, 2, 1, 3)
        .reshape(owners * share, model)
    )


def split_owned(pieces, sizes, size):
    rows = [
        jnp.moveaxis(p.reshape(p.shape[:-1] + (size, p.shape[-1] // size)), -2, 0).reshape(size, -1)
        for p in pieces
    ]
    return jnp.concatenate(rows, axis=1)


def local(
    hidden_in,
    doc_ids,
    attend_weight,
    attend_bias,
    output_weight,
    branch_bias,
    expand_weight,
    expand_bias,
    reduce_weight,
    norm_gain,
    norm_bias,
    out_grad,
):
    size = lax.axis_size("dp")
    layer_count, part, three, width = attend_weight.shape
    tok_rows, model = hidden_in.shape
    share = output_weight.shape[1]
    unit_share = reduce_weight.shape[1]
    hidden_units = expand_weight.shape[2]
    reach_back = (CTX + tok_rows - 2) // tok_rows
    own_row = doc_ids + 1
    mark_list = [passed_along(own_row, "dp", hop) for hop in range(reach_back, 0, -1)]
    marks = (own_row[:, None], jnp.concatenate(mark_list + [own_row])[None, :])

    small_in = (attend_bias, branch_bias, expand_bias, norm_gain, norm_bias)
    flat = jnp.concatenate([entry.reshape(-1) for entry in small_in])
    flat_all = lax.all_gather(flat[None], "dp", axis=0, tiled=True)
    small_full = []
    at = 0
    for entry in small_in:
        piece = flat_all[:, at : at + entry.size].reshape((size,) + entry.shape)
        at += entry.size
        piece = jnp.moveaxis(piece, 0, -2)
        small_full.append(
            piece.reshape(entry.shape[:-1] + (size * entry.shape[-1],)).astype(jnp.float32)
        )
    attend_b, branches, expand_b, gains, offsets = small_full

    params = []
    for layer in range(layer_count):
        first = lax.all_gather(
            jnp.concatenate(
                [
                    attend_weight[layer].reshape(part, three * width),
                    pack_output(output_weight[layer], model, share),
                ],
                axis=1,
            ),
            "dp",
            axis=0,
            tiled=True,
        )
        second = lax.all_gather(
            jnp.concatenate(
                [expand_weight[layer], pack_output(reduce_weight[layer], model, unit_share)],
                axis=1,
            ),
            "dp",
            axis=0,
            tiled=True,
        )
        params.append(
            (
                first[:, : three * width],
                attend_b[layer],
                unpack_output(first[:, three * width :], model, share),
                branches[layer],
                second[:, :hidden_units],
                expand_b[layer],
                unpack_output(second[:, hidden_units:], model, unit_share),
                gains[layer],
                offsets[layer],
            )
        )
    saved = []
    current = hidden_in
    for layer in range(layer_count):
        current, kept_state = forward_layer(current, params[layer], marks, reach_back)
        saved.append(kept_state)
    grad_now = out_grad
    hidden_list = [None] * layer_count
    attend_list = [None] * layer_count
    small_list = [None] * layer_count
    for layer in reversed(range(layer_count)):
        grad_now, expand_grad, reduce_grad, attend_grad, output_grad, small = backward_layer(
            grad_now, params[layer], saved[layer], marks, reach_back
        )
        hidden_list[layer] = scattered(
            jnp.concatenate([expand_grad, pack_output(reduce_grad, model, unit_share)], axis=1)
        )
        small_list[layer] = small
        blocks = [attend_grad, pack_output(output_grad, model, share)]
        if layer == 0:
            stacked = [jnp.stack([entry[i] for entry in small_list]) for i in range(len(small))]
            flat_rows = split_owned(stacked, None, size).astype(jnp.bfloat16)
            count = flat_rows.shape[1]
            room = part * LANES * (-(-count // (part * LANES)))
            padded = jnp.pad(flat_rows, ((0, 0), (0, room - count)))
            blocks.append(padded.reshape(size * part, room // part))
        packed = jnp.concatenate(blocks, axis=1)
        if layer > 0:
            grad_now, packed = lax.optimization_barrier((grad_now, packed))
        attend_list[layer] = scattered(packed)
    hidden_out = [entry.astype(jnp.float32) for entry in hidden_list]
    attend_out = [entry.astype(jnp.float32) for entry in attend_list]
    fold = three * width
    slab = model * share // part
    tail = attend_out[0][:, fold + slab :].reshape(-1)
    small_out = []
    at = 0
    for entry in small_in:
        small_out.append(tail[at : at + entry.size].reshape(entry.shape))
        at += entry.size
    attend_bgrad, branch_bgrad, expand_bgrad, gain_grad, offset_grad = small_out
    return (
        current,
        grad_now,
        jnp.stack([entry[:, :fold].reshape(part, three, width) for entry in attend_out]),
        attend_bgrad,
        jnp.stack([unpack_output(entry[:, fold : fold + slab], model, share) for entry in attend_out]),
        branch_bgrad,
        jnp.stack([entry[:, :hidden_units] for entry in hidden_out]),
        expand_bgrad,
        jnp.stack(
            [unpack_output(entry[:, hidden_units:], model, unit_share) for entry in hidden_out]
        ),
        gain_grad,
        offset_grad,
    )


def solution(mesh):
    return jax.shard_map(
        local,
        mesh=mesh,
        in_specs=(
            P("dp", None),
            P("dp"),
            P(None, "dp", None, "tensor"),
            P(None, None, ("tensor", "dp")),
            P(None, ("tensor", "dp"), None),
            P(None, None, "dp"),
            P(None, "dp", "tensor"),
            P(None, ("tensor", "dp")),
            P(None, ("tensor", "dp"), None),
            P(None, None, "dp"),
            P(None, None, "dp"),
            P("dp", None),
        ),
        out_specs=(
            P("dp", None),
            P("dp", None),
            P(None, "dp", None, "tensor"),
            P(None, None, ("tensor", "dp")),
            P(None, ("tensor", "dp"), None),
            P(None, None, "dp"),
            P(None, "dp", "tensor"),
            P(None, ("tensor", "dp")),
            P(None, ("tensor", "dp"), None),
            P(None, None, "dp"),
            P(None, None, "dp"),
        ),
        check_vma=False,
    )
```
